512 devices in a mesh: row: 16 (over z), col: 32 (over y, x, core).
Axes of the slice: x: 4, y: 4, z: 16, core: 2. Of those that a mesh axis runs over, the one named last changes fastest.
Arguments:
- eigvecs: bfloat16 [8192, 16384], P('row', 'col'), may hold values from -0.01171875 to 0.01171875
- pole_order: int32 [16384], P('col'), may hold values from 0 to 16383, as said below
- pole_weight: float32 [16384], P('col'), may hold values from 0.17 to 6
- root_gap: int32 [2048], replicated, may hold values from 1024 to 15358, as said below
- root_shift: float32 [2048], replicated, may hold values from -0.25 to 0.25
- column_weight: float32 [2048], replicated, may hold values from 4 to 40
- panel_vectors: bfloat16 [2, 8192, 256], P(None, 'row'), may hold values from -0.0625 to 0.0625
- panel_factors: float32 [2, 256, 256], replicated, as said below
Outputs:
- eigenvectors: bfloat16 [8192, 2048], P('row', 'col')
The draws below stay inside these ranges and needn't reach their ends.
Inputs may be any that keep to these rules, and one draw needn't show every extreme that they name: `pole_order`: each value appears once. Distinct values; root j lies strictly between the poles at 2 * root_gap[j] and 2 * root_gap[j] + 2. `panel_factors`: upper triangular, with a diagonal between 2 and 4.
All inputs are finite; a program needn't handle non-finite values.
Results may differ from the reference program's by a relative error of at most 0.02.
Values may be sent and summed in bfloat16 or wider, within the bound.
A program may use at most 64 MiB of HBM per device.

```python
import math
import jax
import jax.numpy as jnp
from jax import lax

K = 16384
EIG = 2048
PW = 256
PANELS = 2
NR = 8192
BLOCK = 32
N_ROW = 16
N_COL = 32


def shared_order(key):
    return jax.random.permutation(jax.random.fold_in(key, 31), K).astype(jnp.int32)


def draw_pole_order(key, part):
    return shared_order(key)


def draw_pole_weight(key, part):
    order = shared_order(key)
    place = order.astype(jnp.float32) / K
    ramp = 0.25 + 4.0 * place * place * place
    factor_key = jax.random.fold_in(key, 32)
    factor = jnp.exp(jax.random.uniform(factor_key, (K,), jnp.float32, math.log(0.7), math.log(1.4)))
    return (ramp * factor).astype(jnp.float32)


def draw_eigvecs(key, part):
    order = shared_order(key)
    place = order.astype(jnp.float32) / K
    freq = jax.random.uniform(jax.random.fold_in(key, 41), (NR, 1), jnp.float32, 0.5, 3.0)
    phase = jax.random.uniform(jax.random.fold_in(key, 42), (NR, 1), jnp.float32, 0.0, 1.0)
    wave = jnp.tanh(4.0 * jnp.sin(2.0 * math.pi * (freq * place[None, :] + phase)))
    spread = jax.random.uniform(jax.random.fold_in(key, 43), (NR, K), jnp.float32, 0.0, 1.0)
    magnitude = 0.5 + spread
    return (wave * magnitude * K ** (-0.5)).astype(jnp.bfloat16)


def draw_root_gap(key, part):
    first_key = jax.random.fold_in(key, 11)
    second_key = jax.random.fold_in(key, 12)
    lowest = K // 16
    highest = K - K // 16 - 2
    inner = jax.random.permutation(first_key, highest - lowest - 1)[:EIG - 2] + lowest + 1
    values = jnp.concatenate([jnp.array([lowest, highest], dtype=jnp.int32), inner.astype(jnp.int32)])
    return jax.random.permutation(second_key, values).astype(jnp.int32)


def draw_panel_factors(key, part):
    first_key = jax.random.fold_in(key, 21)
    second_key = jax.random.fold_in(key, 22)
    diagonal = jax.random.uniform(first_key, (PANELS, PW), jnp.float32, 2.0, 4.0)
    upper = jnp.clip(jax.random.normal(second_key, (PANELS, PW, PW), jnp.float32), -4.0, 4.0)
    upper = jnp.triu(upper * (1.5 / PW ** 0.5), 1)
    eye_table = jnp.eye(PW, dtype=jnp.float32)
    return (upper + diagonal[:, :, None] * eye_table[None, :, :]).astype(jnp.float32)


def levels(rng, dims, shards, least, high):
    gain = 1.0
    for axis_at, parts in shards:
        heights = jax.random.uniform(jax.random.fold_in(jax.random.fold_in(rng, 6), axis_at), (parts,), jnp.float32, least / len(shards), high / len(shards))
        gain = gain * jnp.repeat(jnp.exp(heights), dims[axis_at] // parts).reshape((-1,) + (1,) * (len(dims) - 1 - axis_at))
    return gain


def bell_draw(own_key, shape, width, limit, split=(), kind=jnp.bfloat16):
    values = width * jax.random.normal(own_key, shape, jnp.float32)
    if split:
        values = values * levels(own_key, shape, split, -0.22, 0.18)
    return jnp.clip(values, -limit, limit).astype(kind)


def setup_inputs(seed: int = 0) -> dict:
    seeds = jax.random.split(jax.random.key(seed), 9)
    eigvecs = draw_eigvecs(jax.random.fold_in(seeds[8], 71), 0)
    pole_order = draw_pole_order(jax.random.fold_in(seeds[8], 71), 0)
    pole_weight = draw_pole_weight(jax.random.fold_in(seeds[8], 71), 0)
    root_gap = draw_root_gap(jax.random.fold_in(seeds[8], 71), 0)
    root_shift = jnp.clip(jax.random.uniform(seeds[4], (EIG,), jnp.float32, -0.25, 0.25), -0.25, 0.25)
    column_weight = jnp.clip(jnp.exp(jax.random.uniform(seeds[5], (EIG,), jnp.float32, math.log(4.0), math.log(40.0))), 4.0, 40.0)
    panel_vectors = bell_draw(seeds[6], (PANELS, NR, PW), NR ** -0.5, 0.0625, ((1, 16),))
    panel_factors = draw_panel_factors(jax.random.fold_in(seeds[8], 71), 0)
    return {"eigvecs": eigvecs, "pole_order": pole_order, "pole_weight": pole_weight, "root_gap": root_gap, "root_shift": root_shift, "column_weight": column_weight, "panel_vectors": panel_vectors, "panel_factors": panel_factors}


def cauchy_block(pole_slice, weight_slice, root_gap, root_shift, column_weight):
    pole_values = 2.0 * pole_slice.astype(jnp.float32)
    root_values = 2.0 * root_gap.astype(jnp.float32) + 1.0 + root_shift
    numer = pole_weight_outer(weight_slice, column_weight)
    return (numer / (pole_values[:, None] - root_values[None, :])).astype(jnp.bfloat16)


def pole_weight_outer(weight_slice, column_weight):
    return weight_slice[:, None] * column_weight[None, :]


def reference(eigvecs, pole_order, pole_weight, root_gap, root_shift, column_weight, panel_vectors, panel_factors):
    width_dev = K // N_COL

    def add_block(running, block_index):
        first_pole = (block_index * width_dev).astype(jnp.int32)
        rows_slice = lax.dynamic_slice_in_dim(eigvecs, first_pole, width_dev, 1)
        pole_slice = lax.dynamic_slice_in_dim(pole_order, first_pole, width_dev, 0)
        weight_slice = lax.dynamic_slice_in_dim(pole_weight, first_pole, width_dev, 0)
        matrix = cauchy_block(pole_slice, weight_slice, root_gap, root_shift, column_weight)
        partial_value = jnp.dot(rows_slice, matrix, preferred_element_type=jnp.float32).astype(jnp.bfloat16)
        partial_value = lax.optimization_barrier(partial_value)
        return running + partial_value.astype(jnp.float32), None

    start_sum = jnp.zeros((NR, EIG), jnp.float32)
    summed, unused = lax.scan(add_block, start_sum, jnp.arange(N_COL, dtype=jnp.int32))
    merged = summed.astype(jnp.bfloat16)
    cyclic = merged.reshape(N_ROW, N_ROW, BLOCK, EIG).transpose(1, 0, 2, 3).reshape(NR, EIG)
    current = cyclic.astype(jnp.float32)
    highest = lax.Precision.HIGHEST
    for panel_index in range(PANELS):
        vectors = panel_vectors[panel_index].astype(jnp.float32)
        project = jnp.einsum("rp,rc->pc", vectors, current, precision=highest)
        factored = jnp.dot(panel_factors[panel_index], project, precision=highest)
        current = current - jnp.dot(vectors, factored, precision=highest)
    return current.astype(jnp.bfloat16)
```

```python
import functools

import jax
import jax.numpy as jnp
from jax import lax
from jax.experimental import pallas as pl
from jax.experimental.pallas import tpu as pltpu
from jax.sharding import PartitionSpec as P

MESH = pl.DeviceIdType.MESH
F32, BF16 = jnp.float32, jnp.bfloat16
NZ, NX, NY = 16, 4, 4
NQ = NX * NY
DIST = [8] + [s * d for d in range(7, 0, -1) for s in (1, -1)] + [0]
OFFS = sorted(
    ((dy, dx) for dy in range(NY) for dx in range(NX) if (dy, dx) != (0, 0)),
    key=lambda o: -(min(o[0], NY - o[0]) + min(o[1], NX - o[1])),
)
NT = 4
TA = (((0,), (0,)), ((), ()))


def dot(a, b):
    return jnp.dot(a, b, preferred_element_type=F32)


def kernel(
    a_hbm, order_ref, weight_ref, gap_ref, shift_ref, cw_ref, v_hbm, t_hbm, out_ref,
    a_buf, v_buf, t_buf, pole_b, weight_b, cau, psend, pown, precv, rsend, rrecv, mz, cbuf,
    gf, gs, gr, gall, pf, ps, pr, pall,
    load_sem, pair_s, pair_r, rs_s, rs_r, z_sem, x_sem, g_sem, gx_sem, p_sem,
):
    z = lax.axis_index("row")
    c = lax.axis_index("col")
    core = lax.rem(c, 2)
    q = c // 2
    x, y = lax.rem(q, NX), q // NX
    mate = (z, c + 1 - 2 * core)

    def zpeer(d):
        return lax.rem(z + d + NZ, NZ)

    def chip(off):
        return lax.rem(y + off[0], NY) * NX + lax.rem(x + off[1], NX)

    def send(src, dst, ssem, rsem, dev):
        pltpu.make_async_remote_copy(
            src_ref=src, dst_ref=dst, send_sem=ssem, recv_sem=rsem, device_id=dev, device_id_type=MESH
        ).start()

    def wait(ref, sem):
        pltpu.make_async_copy(ref, ref, sem).wait()

    for j, d in enumerate(DIST):
        for h in range(2):
            half = (1 - core) if h == 0 else core
            start = pl.multiple_of(zpeer(d) * 32 + half * 16, 16)
            pltpu.make_async_copy(
                a_hbm.at[pl.ds(start, 16), :], a_buf.at[j // 4, h, j % 4], load_sem.at[0]
            ).start()
    pltpu.make_async_copy(v_hbm, v_buf, load_sem.at[1]).start()
    pltpu.make_async_copy(t_hbm, t_buf, load_sem.at[2]).start()

    barrier = pltpu.get_barrier_semaphore()
    peers = [(zpeer(d), c) for d in DIST if d] + [(z, chip(o) * 2 + core) for o in OFFS] + [mate]
    for dev in peers:
        pl.semaphore_signal(barrier, inc=1, device_id=dev, device_id_type=MESH)

    for b in range(4):
        lanes = pl.ds(b * 128, 128)
        pole = 2.0 * order_ref[:, lanes].astype(F32)
        pole_b[b] = jnp.broadcast_to(pole, (128, 128)).T
        weight_b[b] = jnp.broadcast_to(weight_ref[:, lanes], (128, 128)).T

    wait(a_buf, load_sem.at[0])

    @pl.loop(0, 8)
    def _(n):
        for e in range(2):
            lanes = pl.ds(pl.multiple_of(n * 256 + e * 128, 128), 128)
            root = 2.0 * gap_ref[:, lanes].astype(F32) + 1.0 + shift_ref[:, lanes]
            for b in range(4):
                cau[b * 128 : b * 128 + 128, e * 128 : e * 128 + 128] = (
                    weight_b[b] / (pole_b[b] - root)
                ).astype(BF16)
        part = dot(a_buf[...].reshape(512, 512), cau[...])
        for t in range(NT):
            for e in range(2):
                lanes = slice(e * 128, e * 128 + 128)
                psend[t, 2 * n + e] = part[t * 128 : t * 128 + 64, lanes].astype(BF16)
                pown[t, 2 * n + e] = part[t * 128 + 64 : t * 128 + 128, lanes]

    wait(v_buf, load_sem.at[1])
    mine = pl.ds(pl.multiple_of(core * 128, 128), 128)
    gram = lax.dot_general(v_buf[1], v_buf[0, :, mine], TA, preferred_element_type=F32)
    gf[...] = gram.reshape(NZ, 16, 128)
    gs[...] = gram.reshape(NZ, 16, 128).astype(BF16)

    pl.semaphore_wait(barrier, len(peers))

    for t in range(NT):
        send(psend.at[t], precv.at[t], pair_s.at[t], pair_r.at[t], mate)
    for j, d in enumerate(DIST[:-1]):
        send(gs.at[zpeer(d)], gr.at[j], g_sem.at[0], g_sem.at[1], (zpeer(d), c))

    for t in range(NT):
        wait(precv.at[t], pair_r.at[t])

        @pl.loop(0, NQ)
        def _(n, t=t):
            rsend[t, n] = (pown[t, n] + precv[t, n].astype(F32)).astype(BF16)

        for j, o in enumerate(OFFS):
            dest = chip(o)
            send(rsend.at[t, dest], rrecv.at[t, j], rs_s.at[t], rs_r.at[t], (z, dest * 2 + core))

    wait(gr, g_sem.at[1])
    total = gf[z]
    for j in range(NZ - 1):
        total += gr[j].astype(F32)
    gall[core, z] = total.astype(BF16)
    for d in DIST[:-1]:
        send(gall.at[core, z], gall.at[core, z], g_sem.at[2], g_sem.at[3], (zpeer(d), c))

    scale = cw_ref[:, pl.ds(pl.multiple_of(q * 128, 128), 128)]
    for t in range(NT):
        wait(rrecv.at[t], rs_r.at[t])
        total = pown[t, q] + precv[t, q].astype(F32)
        for j in range(NQ - 1):
            total += rrecv[t, j].astype(F32)
        merged = (total * scale).astype(BF16)
        for i in range(4):
            d = DIST[4 * t + i]
            if d:
                mz[t, i] = merged[i * 16 : i * 16 + 16]
            else:
                cbuf[core, z] = merged[i * 16 : i * 16 + 16]
        for i in range(4):
            d = DIST[4 * t + i]
            if d:
                send(mz.at[t, i], cbuf.at[core, z], z_sem.at[0], z_sem.at[1], (zpeer(d), c))

    wait(gall.at[0, pl.ds(0, NZ - 1)], g_sem.at[3])
    send(gall.at[core], gall.at[core], gx_sem.at[0], gx_sem.at[1], mate)

    wait(cbuf.at[0, pl.ds(0, NZ - 1)], z_sem.at[1])
    send(cbuf.at[core], cbuf.at[core], x_sem.at[0], x_sem.at[1], mate)
    wait(cbuf.at[0], x_sem.at[1])

    cur = jnp.concatenate([cbuf[k, r] for r in range(NZ) for k in range(2)], axis=0).astype(F32)
    lane = lax.broadcasted_iota(jnp.int32, (512, 128), 1)
    own = jnp.where(lane // 64 == core, cur, pltpu.roll(cur, 64, 1))
    own16 = own.astype(BF16)
    first = lax.dot_general(v_buf[0], own16, TA, preferred_element_type=F32)
    second = lax.dot_general(v_buf[1], own16, TA, preferred_element_type=F32)
    low = lax.broadcasted_iota(jnp.int32, (256, 128), 1) < 64
    proj = jnp.where(low, first, second).reshape(NZ, 16, 128)
    pf[...] = proj
    ps[...] = proj.astype(BF16)
    for j, d in enumerate(DIST[:-1]):
        send(ps.at[zpeer(d)], pr.at[j], p_sem.at[0], p_sem.at[1], (zpeer(d), c))
    wait(pr, p_sem.at[1])
    total = pf[z]
    for j in range(NZ - 1):
        total += pr[j].astype(F32)
    pall[z] = total.astype(BF16)
    for d in DIST[:-1]:
        send(pall.at[z], pall.at[z], p_sem.at[2], p_sem.at[3], (zpeer(d), c))
    wait(t_buf, load_sem.at[2])
    wait(gall.at[0], gx_sem.at[1])
    wait(pall.at[pl.ds(0, NZ - 1)], p_sem.at[3])

    proj16 = pall[...].reshape(256, 128)
    f1 = dot(t_buf[0].astype(BF16), proj16).astype(BF16)
    corr = dot(gall[0].reshape(256, 128), f1[:128]) + dot(gall[1].reshape(256, 128), f1[128:])
    rest = pltpu.roll(proj16.astype(F32), 64, 1) - corr
    f2 = dot(t_buf[1].astype(BF16), rest.astype(BF16)).astype(BF16)
    res = own - dot(v_buf[0], f1) - dot(v_buf[1], f2)
    for b in range(4):
        out_ref[:, b * 128 : b * 128 + 128] = res[b * 128 : b * 128 + 128].T[:64].astype(BF16)

    for t in range(NT):
        wait(psend.at[t], pair_s.at[t])
        wait(rrecv.at[t], rs_s.at[t])
    wait(gr, g_sem.at[0])
    wait(gr, g_sem.at[2])
    wait(gall.at[0], gx_sem.at[0])
    wait(gr, z_sem.at[0])
    wait(cbuf.at[0], x_sem.at[0])
    wait(pr, p_sem.at[0])
    wait(pr, p_sem.at[2])


def shards(a, order, weight, gap, shift, cw, v, t):
    vmem = pl.BlockSpec(memory_space=pltpu.VMEM)
    hbm = pl.BlockSpec(memory_space=pl.ANY)
    dma = pltpu.SemaphoreType.DMA
    out = pl.pallas_call(
        kernel,
        out_shape=jax.ShapeDtypeStruct((64, 512), BF16),
        in_specs=[hbm, vmem, vmem, vmem, vmem, vmem, hbm, hbm],
        out_specs=vmem,
        scratch_shapes=[
            pltpu.VMEM((NT, 2, 4, 16, 512), BF16),
            pltpu.VMEM((2, 512, 256), BF16),
            pltpu.VMEM((2, 256, 256), F32),
            pltpu.VMEM((4, 128, 128), F32),
            pltpu.VMEM((4, 128, 128), F32),
            pltpu.VMEM((512, 256), BF16),
            pltpu.VMEM((NT, NQ, 64, 128), BF16),
            pltpu.VMEM((NT, NQ, 64, 128), F32),
            pltpu.VMEM((NT, NQ, 64, 128), BF16),
            pltpu.VMEM((NT, NQ, 64, 128), BF16),
            pltpu.VMEM((NT, NQ - 1, 64, 128), BF16),
            pltpu.VMEM((NT, 4, 16, 128), BF16),
            pltpu.VMEM((2, NZ, 16, 128), BF16),
            pltpu.VMEM((NZ, 16, 128), F32),
            pltpu.VMEM((NZ, 16, 128), BF16),
            pltpu.VMEM((NZ - 1, 16, 128), BF16),
            pltpu.VMEM((2, NZ, 16, 128), BF16),
            pltpu.VMEM((NZ, 16, 128), F32),
            pltpu.VMEM((NZ, 16, 128), BF16),
            pltpu.VMEM((NZ - 1, 16, 128), BF16),
            pltpu.VMEM((NZ, 16, 128), BF16),
            dma((3,)), dma((NT,)), dma((NT,)), dma((NT,)), dma((NT,)),
            dma((2,)), dma((2,)), dma((4,)), dma((2,)), dma((4,)),
        ],
        compiler_params=pltpu.CompilerParams(collective_id=0, has_side_effects=True),
    )(
        a, order.reshape(1, -1), weight.reshape(1, -1), gap.reshape(1, -1), shift.reshape(1, -1),
        cw.reshape(1, -1), v, t,
    )
    return out.T


def solution(mesh):
    return jax.shard_map(
        shards,
        mesh=mesh,
        in_specs=(P("row", "col"), P("col"), P("col"), P(), P(), P(), P(None, "row", None), P()),
        out_specs=P("row", "col"),
        check_vma=False,
    )
```

```python
import jax
import jax.numpy as jnp
from jax import lax
from jax.experimental import pallas as pl
from jax.experimental.pallas import tpu as pltpu
from jax.sharding import PartitionSpec as P

MESH = pl.DeviceIdType.MESH
F32, BF16 = jnp.float32, jnp.bfloat16
NZ, NX, NY = 16, 4, 4
NQ = NX * NY
DIST = [8] + [s * d for d in range(7, 0, -1) for s in (1, -1)] + [0]
NEAR = [4, 3, -3, 2, -2, 1, -1]
NT = 4
TA = (((0,), (0,)), ((), ()))


def dot(a, b):
    return jnp.dot(a, b, preferred_element_type=F32)


def kernel(
    a_hbm, order_hbm, weight_hbm, gap_hbm, shift_hbm, cw_hbm, v_hbm, t_hbm, out_ref,
    order_ref, weight_ref, gap_ref, shift_ref, cw_ref, a_buf, v_buf, t_buf, vt,
    pole_b, weight_b, cau, part, precv, s1, r1, s2, r2, mz, cbuf,
    gf, gsum, gin, gall, w1, w2, own_t, pf, ps, pr, pall,
    load_sem, pair_s, pair_r, s1_s, s1_r, s2_s, s2_r, z_sem, g_sem, gx_sem, p_sem, tok,
):
    z = lax.axis_index("row")
    c = lax.axis_index("col")
    core = c & 1
    q = c >> 1
    x, y = q & (NX - 1), q >> 2
    mate = (z, c + 1 - 2 * core)

    def zpeer(d):
        return (z + d + NZ) & (NZ - 1)

    def xchip(d):
        return (y * NX + ((x + d) & (NX - 1))) * 2 + core

    def ychip(d):
        return (((y + d) & (NY - 1)) * NX + x) * 2 + core

    def send(src, dst, ssem, rsem, dev):
        pltpu.make_async_remote_copy(
            src_ref=src, dst_ref=dst, send_sem=ssem, recv_sem=rsem, device_id=dev, device_id_type=MESH
        ).start()

    def wait(ref, sem):
        pltpu.make_async_copy(ref, ref, sem).wait()

    small = [
        (order_hbm, order_ref), (weight_hbm, weight_ref), (gap_hbm, gap_ref),
        (shift_hbm, shift_ref), (cw_hbm, cw_ref),
    ]
    for i, (src, dst) in enumerate(small):
        pltpu.make_async_copy(src, dst, load_sem.at[3 + i]).start()
    barrier = pltpu.get_barrier_semaphore()
    peers = [mate]
    for d in (1, 2, 3):
        peers += [(z, xchip(d)), (z, ychip(d))]
    peers += [(zpeer(d), c) for d in (1, -1)]
    for dev in peers:
        pl.semaphore_signal(barrier, inc=1, device_id=dev, device_id_type=MESH)

    for j, d in enumerate(DIST):
        pltpu.make_async_copy(a_hbm.at[zpeer(d)], a_buf.at[j // 4, :, j % 4], load_sem.at[0]).start()

    for i in range(4):
        wait(small[i][1], load_sem.at[3 + i])
    pltpu.make_async_copy(v_hbm, v_buf, load_sem.at[1]).start()
    pltpu.make_async_copy(t_hbm, t_buf, load_sem.at[2]).start()
    for b in range(4):
        lanes = pl.ds(b * 128, 128)
        pole = 2.0 * order_ref[:, lanes].astype(F32)
        pole_b[b] = jnp.broadcast_to(pole, (128, 128)).T
        weight_b[b] = jnp.broadcast_to(weight_ref[:, lanes], (128, 128)).T

    root = 2.0 * gap_ref[...].astype(F32) + 1.0 + shift_ref[...]
    turned_root = pltpu.roll(root, 64, 1)
    left1 = lax.broadcasted_iota(jnp.int32, (1, 128), 1) < 64

    def cauchy(n):
        for e in range(4):
            b0 = 2 * (4 * (n % 2) + e)
            if n < 2:
                lanes = jnp.where(left1, root[b0 : b0 + 1], turned_root[b0 + 1 : b0 + 2])
            else:
                lanes = jnp.where(left1, turned_root[b0 : b0 + 1], root[b0 + 1 : b0 + 2])
            for b in range(4):
                cau[n, b * 128 : b * 128 + 128, e * 128 : e * 128 + 128] = (
                    weight_b[b] / (pole_b[b] - lanes)
                ).astype(BF16)

    for n in range(4):
        cauchy(n)
    wait(a_buf, load_sem.at[0])
    for t in range(NT):
        for n in range(4):
            prod = dot(a_buf[t].reshape(128, 512), cau[n]).astype(BF16)
            for e in range(4):
                part[n // 2, t, 4 * (n % 2) + e] = prod[:, e * 128 : e * 128 + 128]
        if t == 0:
            pl.semaphore_wait(barrier, len(peers))
        send(part.at[1 - core, t], precv.at[t], pair_s.at[t], pair_r.at[t], mate)
    token(tok, 0, (1, -1), zpeer, c)

    wait(v_buf, load_sem.at[1])
    mine = pl.ds(pl.multiple_of(core * 128, 128), 128)
    gram = lax.dot_general(v_buf[1], v_buf[0, :, mine], TA, preferred_element_type=F32)
    gf[...] = gram.reshape(NQ, 16, 128)
    gsum[0] = gf[q]

    def gram_send(i):
        for j in range(3):
            to = zpeer((1 - 2 * core) * (j + 1) * 4**i)
            send(gsum.at[i], gin.at[i, j], g_sem.at[i], g_sem.at[2 + i], (to, c))

    def gram_add(i):
        wait(gin.at[i], g_sem.at[2 + i])
        gsum[i + 1] = gsum[i] + gin[i, 0] + gin[i, 1] + gin[i, 2]

    left64 = lax.broadcasted_iota(jnp.int32, (64, 128), 1) < 64

    def first_phase(t):
        wait(precv.at[t], pair_r.at[t])

        @pl.loop(0, NY)
        def _(yy):
            for e in range(2):
                total = part[core, t, 2 * yy + e].astype(F32) + precv[t, 2 * yy + e].astype(F32)
                turned = pltpu.roll(total, 64, 1)
                even = jnp.where(left64, total[:64], turned[64:]).astype(BF16)
                odd = jnp.where(left64, turned[:64], total[64:]).astype(BF16)
                for xx, packed in ((2 * e, even), (2 * e + 1, odd)):
                    s1[t, 0, xx, yy] = packed[:32]
                    s1[t, 1, yy, xx] = packed[32:]

    def first_sends(t, ds):
        for d in ds:
            send(s1.at[t, 0, (x + d) & (NX - 1)], r1.at[t, 0, d - 1], s1_s.at[t], s1_r.at[t], (z, xchip(d)))
            send(s1.at[t, 1, (y + d) & (NY - 1)], r1.at[t, 1, d - 1], s1_s.at[t], s1_r.at[t], (z, ychip(d)))

    def second_phase(t):
        wait(r1.at[t], s1_r.at[t])
        for h, me in ((0, x), (1, y)):
            total = s1[t, h, me].astype(F32)
            for j in range(3):
                total += r1[t, h, j].astype(F32)
            s2[t, h] = total.astype(BF16)
        for d in (2, 1, 3):
            send(s2.at[t, 0, ((y + d) & (NY - 1))], r2.at[t, 0, d - 1], s2_s.at[t], s2_r.at[t], (z, ychip(d)))
            send(s2.at[t, 1, ((x + d) & (NX - 1))], r2.at[t, 1, d - 1], s2_s.at[t], s2_r.at[t], (z, xchip(d)))

    def exchange(t):
        wait(r2.at[t], s2_r.at[t])
        for h, me in ((0, y), (1, x)):
            total = s2[t, h, me].astype(F32)
            for j in range(3):
                total += r2[t, h, j].astype(F32)
            mz[t, 2 * h : 2 * h + 2] = (total * scale).astype(BF16).reshape(2, 16, 128)
        for i in range(4):
            d = DIST[4 * t + i]
            if d:
                send(mz.at[t, i], cbuf.at[z], z_sem.at[0], z_sem.at[1], (zpeer(d), c))
            else:
                cbuf[z] = mz[t, i]

    first_phase(0)
    first_sends(0, (2, 1, 3))
    first_phase(1)
    first_sends(1, (2, 1, 3))
    pl.semaphore_wait(tok.at[0], 2)
    token(tok, 1, (2, -2), zpeer, c)
    first_phase(2)
    first_sends(2, (2,))
    first_phase(3)
    second_phase(0)
    first_sends(2, (1, 3))
    first_sends(3, (2, 1, 3))
    pl.semaphore_wait(tok.at[1], 2)
    token(tok, 2, (4, -4), zpeer, c)
    gram_send(0)
    second_phase(1)
    wait(cw_ref, load_sem.at[7])
    cw = cw_ref[pl.ds(q, 1), :]
    scale = jnp.where(lax.broadcasted_iota(jnp.int32, (1, 128), 1) // 64 == core, cw, pltpu.roll(cw, 64, 1))
    pl.semaphore_wait(tok.at[2], 2)
    exchange(0)
    second_phase(2)
    exchange(1)
    gram_add(0)
    gram_send(1)
    second_phase(3)
    exchange(2)
    for p in range(2):
        vt[p] = v_buf[p].T
    exchange(3)
    wait(t_buf, load_sem.at[2])
    w2[...] = lax.dot_general(t_buf[1].astype(BF16), vt[1], TA, preferred_element_type=F32).astype(BF16)

    wait(cbuf.at[pl.ds(0, NZ - 1)], z_sem.at[1])
    cur = cbuf[...].astype(F32)
    turned = pltpu.roll(cur.reshape(256, 128), 64, 1).reshape(NZ, 16, 128)
    left = lax.broadcasted_iota(jnp.int32, (NZ, 16, 128), 2) < 64
    own = jnp.stack([jnp.where(left, cur, turned), jnp.where(left, turned, cur)], axis=1).reshape(512, 128)
    own16 = own.astype(BF16)
    low = lax.broadcasted_iota(jnp.int32, (256, 128), 1) < 64
    proj = jnp.where(low, dot(vt[0], own16), dot(vt[1], own16)).reshape(8, 32, 128)
    pf[...] = proj
    ps[...] = proj.astype(BF16)
    for j, d in enumerate(NEAR):
        send(ps.at[zpeer(d) & 7], pr.at[j], p_sem.at[0], p_sem.at[1], (zpeer(d), c))

    for b in range(4):
        own_t[:, b * 128 : b * 128 + 128] = own[b * 128 : b * 128 + 128].T[:64]
    gram_add(1)
    gall[core, q] = gsum[2].astype(BF16)
    for dy in range(NY):
        for dx in range(NX):
            if dx or dy:
                dest = (((y + dy) & (NY - 1)) * NX + ((x + dx) & (NX - 1))) * 2 + core
                send(gall.at[core, q], gall.at[core, q], g_sem.at[4], g_sem.at[5], (z, dest))

    wait(pr, p_sem.at[1])
    total = pf[z & 7]
    for j in range(len(NEAR)):
        total += pr[j].astype(F32)
    pall[z] = total.astype(BF16)
    for d in DIST[:-1]:
        send(pall.at[z], pall.at[z], p_sem.at[2], p_sem.at[3], (zpeer(d), c))
    wait(gall.at[0, pl.ds(0, NQ - 1)], g_sem.at[5])
    send(gall.at[core], gall.at[core], gx_sem.at[0], gx_sem.at[1], mate)
    wait(gall.at[0], gx_sem.at[1])
    rest = jnp.concatenate(
        [
            lax.dot_general(gall[k].reshape(256, 128), w2[...], TA, preferred_element_type=F32)
            for k in range(2)
        ],
        axis=0,
    )
    rest = (vt[0].astype(F32) - rest).astype(BF16)
    w1[...] = lax.dot_general(t_buf[0].astype(BF16), rest, TA, preferred_element_type=F32).astype(BF16)

    for t in range(NT):
        wait(precv.at[t], pair_s.at[t])
        wait(r1.at[t], s1_s.at[t])
        wait(r2.at[t], s2_s.at[t])
    for i in range(2):
        wait(gin.at[i], g_sem.at[i])
    wait(gall.at[0, pl.ds(0, NQ - 1)], g_sem.at[4])
    wait(gall.at[0], gx_sem.at[0])
    wait(cbuf.at[pl.ds(0, NZ - 1)], z_sem.at[0])
    wait(pr, p_sem.at[0])
    wait(pall.at[pl.ds(0, NZ - 1)], p_sem.at[2])
    wait(pall.at[pl.ds(0, NZ - 1)], p_sem.at[3])
    proj = (pall[:8].astype(F32) + pall[8:].astype(F32)).reshape(256, 128).T.astype(BF16)
    out_ref[...] = (own_t[...] - (dot(proj[:64], w1[...]) + dot(proj[64:], w2[...]))).astype(BF16)


def token(tok, at, steps, zpeer, c):
    for d in steps:
        pl.semaphore_signal(tok.at[at], inc=1, device_id=(zpeer(d), c), device_id_type=MESH)


def shards(a, order, weight, gap, shift, cw, v, t):
    hbm = pl.BlockSpec(memory_space=pl.ANY)
    dma = pltpu.SemaphoreType.DMA
    vmem = pltpu.VMEM
    out = pl.pallas_call(
        kernel,
        out_shape=vmem((64, 512), BF16),
        in_specs=[hbm] * 8,
        out_specs=pl.BlockSpec(memory_space=pltpu.VMEM),
        scratch_shapes=[
            vmem((1, 512), jnp.int32), vmem((1, 512), F32), vmem((NQ, 128), jnp.int32),
            vmem((NQ, 128), F32), vmem((NQ, 128), F32),
            vmem((NT, 2, 4, 16, 512), BF16),
            vmem((2, 512, 256), BF16),
            vmem((2, 256, 256), F32),
            vmem((2, 256, 512), BF16),
            vmem((4, 128, 128), F32),
            vmem((4, 128, 128), F32),
            vmem((4, 512, 512), BF16),
            vmem((2, NT, 8, 128, 128), BF16),
            vmem((NT, 8, 128, 128), BF16),
            vmem((NT, 2, 4, 4, 32, 128), BF16),
            vmem((NT, 2, 3, 4, 32, 128), BF16),
            vmem((NT, 2, 4, 32, 128), BF16),
            vmem((NT, 2, 3, 32, 128), BF16),
            vmem((NT, 4, 16, 128), BF16),
            vmem((NZ, 16, 128), BF16),
            vmem((NQ, 16, 128), F32),
            vmem((3, 16, 128), F32),
            vmem((2, 3, 16, 128), F32),
            vmem((2, NQ, 16, 128), BF16),
            vmem((256, 512), BF16),
            vmem((256, 512), BF16),
            vmem((64, 512), F32),
            vmem((8, 32, 128), F32),
            vmem((8, 32, 128), BF16),
            vmem((7, 32, 128), BF16),
            vmem((NZ, 32, 128), BF16),
            dma((8,)), dma((NT,)), dma((NT,)), dma((NT,)), dma((NT,)), dma((NT,)), dma((NT,)),
            dma((2,)), dma((10,)), dma((2,)), dma((4,)), pltpu.SemaphoreType.REGULAR((3,)),
        ],
        compiler_params=pltpu.CompilerParams(collective_id=0, has_side_effects=True),
    )(
        a.reshape(NZ, 2, 16, 512), order.reshape(1, -1), weight.reshape(1, -1), gap.reshape(NQ, 128),
        shift.reshape(NQ, 128), cw.reshape(NQ, 128), v, t,
    )
    return out.T


def solution(mesh):
    return jax.shard_map(
        shards,
        mesh=mesh,
        in_specs=(P("row", "col"), P("col"), P("col"), P(), P(), P(), P(None, "row", None), P()),
        out_specs=P("row", "col"),
        check_vma=False,
    )
```

```python
import jax
import jax.numpy as jnp
from jax import lax
from jax.experimental import pallas as pl
from jax.experimental.pallas import tpu as pltpu
from jax.sharding import PartitionSpec as P

MESH = pl.DeviceIdType.MESH
F32, BF16 = jnp.float32, jnp.bfloat16
NZ, NX, NY = 16, 4, 4
NQ = NX * NY
DIST = [8] + [s * d for d in range(7, 0, -1) for s in (1, -1)] + [0]
GATHER = [0, 1, 2, 3, 4, 5, 6, 15, 14, 7, 13, 12, 11, 8, 10, 9]
OWNERS = [4, 13, 3, 14, 2, 15, 1, 0]
NT = 4
TA = (((0,), (0,)), ((), ()))


def dot(a, b):
    return jnp.dot(a, b, preferred_element_type=F32)


def kernel(
    a_hbm, order_hbm, weight_hbm, gap_hbm, shift_hbm, cw_hbm, v_hbm, t_hbm, out_ref,
    order_ref, weight_ref, gap_ref, shift_ref, cw_ref, a_buf, v_buf, t_buf, vt,
    pole_b, weight_b, cau, part, precv, s1, r1, s2, r2, mz, cbuf,
    gf, gsum, gin, gall, w1, w2, own_t, pf, ps, pr, pall,
    load_sem, pair_s, pair_r, s1_s, s1_r, s2_s, s2_r, z_sem, g_sem, gx_sem, p_sem, tok,
):
    z = lax.axis_index("row")
    c = lax.axis_index("col")
    core = c & 1
    q = c >> 1
    x, y = q & (NX - 1), q >> 2
    mate = (z, c + 1 - 2 * core)

    def zpeer(d):
        return (z + d + NZ) & (NZ - 1)

    def xchip(d):
        return (y * NX + ((x + d) & (NX - 1))) * 2 + core

    def ychip(d):
        return (((y + d) & (NY - 1)) * NX + x) * 2 + core

    def send(src, dst, ssem, rsem, dev):
        pltpu.make_async_remote_copy(
            src_ref=src, dst_ref=dst, send_sem=ssem, recv_sem=rsem, device_id=dev, device_id_type=MESH
        ).start()

    def wait(ref, sem):
        pltpu.make_async_copy(ref, ref, sem).wait()

    small = [
        (order_hbm, order_ref), (weight_hbm, weight_ref), (gap_hbm, gap_ref),
        (shift_hbm, shift_ref), (cw_hbm, cw_ref),
    ]
    for i, (src, dst) in enumerate(small):
        pltpu.make_async_copy(src, dst, load_sem.at[3 + i]).start()
    barrier = pltpu.get_barrier_semaphore()
    peers = [mate]
    for d in (1, 2, 3):
        peers += [(z, xchip(d)), (z, ychip(d))]
    peers += [(zpeer(d), c) for d in (1, -1)]
    for dev in peers:
        pl.semaphore_signal(barrier, inc=1, device_id=dev, device_id_type=MESH)

    for j, d in enumerate(DIST):
        pltpu.make_async_copy(a_hbm.at[zpeer(d)], a_buf.at[j // 4, :, j % 4], load_sem.at[0]).start()

    for i in range(4):
        wait(small[i][1], load_sem.at[3 + i])
    pltpu.make_async_copy(v_hbm, v_buf, load_sem.at[1]).start()
    pltpu.make_async_copy(t_hbm, t_buf, load_sem.at[2]).start()
    for b in range(4):
        lanes = pl.ds(b * 128, 128)
        pole = 2.0 * order_ref[:, lanes].astype(F32)
        pole_b[b] = jnp.broadcast_to(pole, (128, 128)).T
        weight_b[b] = jnp.broadcast_to(weight_ref[:, lanes], (128, 128)).T

    root = 2.0 * gap_ref[...].astype(F32) + 1.0 + shift_ref[...]
    turned_root = pltpu.roll(root, 64, 1)
    left1 = lax.broadcasted_iota(jnp.int32, (1, 128), 1) < 64

    def cauchy(n):
        for e in range(4):
            b0 = 2 * (4 * (n % 2) + e)
            if n < 2:
                lanes = jnp.where(left1, root[b0 : b0 + 1], turned_root[b0 + 1 : b0 + 2])
            else:
                lanes = jnp.where(left1, turned_root[b0 : b0 + 1], root[b0 + 1 : b0 + 2])
            for b in range(4):
                cau[n, b * 128 : b * 128 + 128, e * 128 : e * 128 + 128] = (
                    weight_b[b] / (pole_b[b] - lanes)
                ).astype(BF16)

    for n in range(4):
        cauchy(n)
    wait(a_buf, load_sem.at[0])
    for t in range(NT):
        for n in range(4):
            prod = dot(a_buf[t].reshape(128, 512), cau[n]).astype(BF16)
            for e in range(4):
                part[n // 2, t, 4 * (n % 2) + e] = prod[:, e * 128 : e * 128 + 128]
        if t == 0:
            pl.semaphore_wait(barrier, len(peers))
        send(part.at[1 - core, t], precv.at[t], pair_s.at[t], pair_r.at[t], mate)
    token(tok, 0, (1, -1), zpeer, c)

    wait(v_buf, load_sem.at[1])
    mine = pl.ds(pl.multiple_of(core * 128, 128), 128)
    gram = lax.dot_general(v_buf[1], v_buf[0, :, mine], TA, preferred_element_type=F32)
    gf[...] = gram.reshape(NQ, 16, 128)
    gsum[0] = gf[q]

    def gram_send(i):
        for j in range(3):
            to = zpeer((1 - 2 * core) * (j + 1) * 4**i)
            send(gsum.at[i], gin.at[i, j], g_sem.at[i], g_sem.at[2 + i], (to, c))

    def gram_add(i):
        wait(gin.at[i], g_sem.at[2 + i])
        gsum[i + 1] = gsum[i] + gin[i, 0] + gin[i, 1] + gin[i, 2]

    left64 = lax.broadcasted_iota(jnp.int32, (64, 128), 1) < 64

    def first_phase(t):
        wait(precv.at[t], pair_r.at[t])

        for yy in range(NY):
            for e in range(2):
                total = part[core, t, 2 * yy + e].astype(F32) + precv[t, 2 * yy + e].astype(F32)
                turned = pltpu.roll(total, 64, 1)
                even = jnp.where(left64, total[:64], turned[64:]).astype(BF16)
                odd = jnp.where(left64, turned[:64], total[64:]).astype(BF16)
                for xx, packed in ((2 * e, even), (2 * e + 1, odd)):
                    s1[t, 0, xx, yy] = packed[:32]
                    s1[t, 1, yy, xx] = packed[32:]

    def first_sends(t, ds):
        for d in ds:
            send(s1.at[t, 0, (x + d) & (NX - 1)], r1.at[t, 0, d - 1], s1_s.at[t], s1_r.at[t], (z, xchip(d)))
            send(s1.at[t, 1, (y + d) & (NY - 1)], r1.at[t, 1, d - 1], s1_s.at[t], s1_r.at[t], (z, ychip(d)))

    def second_phase(t):
        wait(r1.at[t], s1_r.at[t])
        for h, me in ((0, x), (1, y)):
            total = s1[t, h, me].astype(F32)
            for j in range(3):
                total += r1[t, h, j].astype(F32)
            s2[t, h] = total.astype(BF16)
        for d in (2, 1, 3):
            send(s2.at[t, 0, ((y + d) & (NY - 1))], r2.at[t, 0, d - 1], s2_s.at[t], s2_r.at[t], (z, ychip(d)))
            send(s2.at[t, 1, ((x + d) & (NX - 1))], r2.at[t, 1, d - 1], s2_s.at[t], s2_r.at[t], (z, xchip(d)))

    def exchange(t):
        wait(r2.at[t], s2_r.at[t])
        for h, me in ((0, y), (1, x)):
            total = s2[t, h, me].astype(F32)
            for j in range(3):
                total += r2[t, h, j].astype(F32)
            mz[t, 2 * h : 2 * h + 2] = (total * scale).astype(BF16).reshape(2, 16, 128)
        for i in range(4):
            d = DIST[4 * t + i]
            if d:
                send(mz.at[t, i], cbuf.at[z], z_sem.at[0], z_sem.at[1], (zpeer(d), c))
            else:
                cbuf[z] = mz[t, i]

    for t in range(3):
        first_phase(t)
        first_sends(t, (2, 1, 3))
    pl.semaphore_wait(tok.at[0], 2)
    token(tok, 1, (2, -2), zpeer, c)
    second_phase(0)
    first_phase(3)
    first_sends(3, (2, 1, 3))
    pl.semaphore_wait(tok.at[1], 2)
    token(tok, 2, (4, -4), zpeer, c)
    gram_send(0)
    second_phase(1)
    wait(cw_ref, load_sem.at[7])
    cw = cw_ref[pl.ds(q, 1), :]
    scale = jnp.where(lax.broadcasted_iota(jnp.int32, (1, 128), 1) // 64 == core, cw, pltpu.roll(cw, 64, 1))
    pl.semaphore_wait(tok.at[2], 2)
    exchange(0)
    second_phase(2)
    exchange(1)
    gram_add(0)
    gram_send(1)
    second_phase(3)
    exchange(2)
    exchange(3)
    for p in range(2):
        vt[p] = v_buf[p].T
    wait(t_buf, load_sem.at[2])
    w2[...] = lax.dot_general(t_buf[1].astype(BF16), vt[1], TA, preferred_element_type=F32).astype(BF16)

    wait(cbuf.at[pl.ds(0, NZ - 1)], z_sem.at[1])
    cur = cbuf[...].astype(F32)
    turned = pltpu.roll(cur.reshape(256, 128), 64, 1).reshape(NZ, 16, 128)
    left = lax.broadcasted_iota(jnp.int32, (NZ, 16, 128), 2) < 64
    own = jnp.stack([jnp.where(left, cur, turned), jnp.where(left, turned, cur)], axis=1).reshape(512, 128)
    own16 = own.astype(BF16)
    low = lax.broadcasted_iota(jnp.int32, (256, 128), 1) < 64
    proj = jnp.where(low, dot(vt[0], own16), dot(vt[1], own16)).reshape(8, 32, 128)
    pf[...] = proj
    ps[...] = proj.astype(BF16)
    slot = (z + 3) & (NZ - 1)
    for owner in OWNERS:

        @pl.when(z != owner)
        def _(owner=owner):
            send(
                ps.at[(owner + 3) % NZ], pr.at[(z - owner - 1 + NZ) & (NZ - 1)],
                p_sem.at[0], p_sem.at[1], (owner, c),
            )


    for b in range(4):
        own_t[:, b * 128 : b * 128 + 128] = own[b * 128 : b * 128 + 128].T[:64]
    gram_add(1)
    gall[core, q] = gsum[2].astype(BF16)
    for dy in range(NY):
        for dx in range(NX):
            if dx or dy:
                dest = (((y + dy) & (NY - 1)) * NX + ((x + dx) & (NX - 1))) * 2 + core
                send(gall.at[core, q], gall.at[core, q], g_sem.at[4], g_sem.at[5], (z, dest))

    @pl.when(slot < 8)
    def _():
        wait(pr, p_sem.at[1])
        total = pf[slot]
        for j in range(NZ - 1):
            total += pr[j].astype(F32)
        pall[slot] = total.astype(BF16)
        for dest in GATHER:

            @pl.when(z != dest)
            def _(dest=dest):
                send(pall.at[slot], pall.at[slot], p_sem.at[2], p_sem.at[3], (dest, c))

    wait(gall.at[0, pl.ds(0, NQ - 1)], g_sem.at[5])
    send(gall.at[core], gall.at[core], gx_sem.at[0], gx_sem.at[1], mate)
    wait(gall.at[0], gx_sem.at[1])
    rest = jnp.concatenate(
        [
            lax.dot_general(gall[k].reshape(256, 128), w2[...], TA, preferred_element_type=F32)
            for k in range(2)
        ],
        axis=0,
    )
    rest = (vt[0].astype(F32) - rest).astype(BF16)
    w1[...] = lax.dot_general(t_buf[0].astype(BF16), rest, TA, preferred_element_type=F32).astype(BF16)

    for t in range(NT):
        wait(precv.at[t], pair_s.at[t])
        wait(r1.at[t], s1_s.at[t])
        wait(r2.at[t], s2_s.at[t])
    for i in range(2):
        wait(gin.at[i], g_sem.at[i])
    wait(gall.at[0, pl.ds(0, NQ - 1)], g_sem.at[4])
    wait(gall.at[0], gx_sem.at[0])
    wait(cbuf.at[pl.ds(0, NZ - 1)], z_sem.at[0])

    @pl.when(slot < 8)
    def _():
        wait(pr.at[pl.ds(0, 7)], p_sem.at[0])
        wait(pr, p_sem.at[2])
        wait(pall.at[pl.ds(0, 7)], p_sem.at[3])

    @pl.when(slot >= 8)
    def _():
        wait(pr.at[pl.ds(0, 8)], p_sem.at[0])
        wait(pall, p_sem.at[3])

    proj = pall[...].reshape(256, 128).T
    out_ref[...] = (own_t[...] - (dot(proj[:64], w1[...]) + dot(proj[64:], w2[...]))).astype(BF16)


def token(tok, at, steps, zpeer, c):
    for d in steps:
        pl.semaphore_signal(tok.at[at], inc=1, device_id=(zpeer(d), c), device_id_type=MESH)


def shards(a, order, weight, gap, shift, cw, v, t):
    hbm = pl.BlockSpec(memory_space=pl.ANY)
    dma = pltpu.SemaphoreType.DMA
    vmem = pltpu.VMEM
    out = pl.pallas_call(
        kernel,
        out_shape=vmem((64, 512), BF16),
        in_specs=[hbm] * 8,
        out_specs=pl.BlockSpec(memory_space=pltpu.VMEM),
        scratch_shapes=[
            vmem((1, 512), jnp.int32), vmem((1, 512), F32), vmem((NQ, 128), jnp.int32),
            vmem((NQ, 128), F32), vmem((NQ, 128), F32),
            vmem((NT, 2, 4, 16, 512), BF16),
            vmem((2, 512, 256), BF16),
            vmem((2, 256, 256), F32),
            vmem((2, 256, 512), BF16),
            vmem((4, 128, 128), F32),
            vmem((4, 128, 128), F32),
            vmem((4, 512, 512), BF16),
            vmem((2, NT, 8, 128, 128), BF16),
            vmem((NT, 8, 128, 128), BF16),
            vmem((NT, 2, 4, 4, 32, 128), BF16),
            vmem((NT, 2, 3, 4, 32, 128), BF16),
            vmem((NT, 2, 4, 32, 128), BF16),
            vmem((NT, 2, 3, 32, 128), BF16),
            vmem((NT, 4, 16, 128), BF16),
            vmem((NZ, 16, 128), BF16),
            vmem((NQ, 16, 128), F32),
            vmem((3, 16, 128), F32),
            vmem((2, 3, 16, 128), F32),
            vmem((2, NQ, 16, 128), BF16),
            vmem((256, 512), BF16),
            vmem((256, 512), BF16),
            vmem((64, 512), F32),
            vmem((8, 32, 128), F32),
            vmem((8, 32, 128), BF16),
            vmem((NZ - 1, 32, 128), BF16),
            vmem((8, 32, 128), BF16),
            dma((8,)), dma((NT,)), dma((NT,)), dma((NT,)), dma((NT,)), dma((NT,)), dma((NT,)),
            dma((2,)), dma((10,)), dma((2,)), dma((4,)), pltpu.SemaphoreType.REGULAR((3,)),
        ],
        compiler_params=pltpu.CompilerParams(collective_id=0, has_side_effects=True),
    )(
        a.reshape(NZ, 2, 16, 512), order.reshape(1, -1), weight.reshape(1, -1), gap.reshape(NQ, 128),
        shift.reshape(NQ, 128), cw.reshape(NQ, 128), v, t,
    )
    return out.T


def solution(mesh):
    return jax.shard_map(
        shards,
        mesh=mesh,
        in_specs=(P("row", "col"), P("col"), P("col"), P(), P(), P(), P(None, "row", None), P()),
        out_specs=P("row", "col"),
        check_vma=False,
    )
```

```python
import jax
import jax.numpy as jnp
from jax import lax
from jax.experimental import pallas as pl
from jax.experimental.pallas import tpu as pltpu
from jax.sharding import PartitionSpec as P

MESH = pl.DeviceIdType.MESH
F32, BF16 = jnp.float32, jnp.bfloat16
NZ, NX, NY = 16, 4, 4
NQ = NX * NY
DIST = [8] + [s * d for d in range(7, 0, -1) for s in (1, -1)] + [0]
GATHER = [0, 1, 2, 3, 4, 5, 6, 15, 14, 7, 13, 12, 11, 8, 10, 9]
OWNERS = [4, 13, 3, 14, 2, 15, 1, 0]
NT = 4
TA = (((0,), (0,)), ((), ()))


def dot(a, b):
    return jnp.dot(a, b, preferred_element_type=F32)


def kernel(
    a_hbm, order_hbm, weight_hbm, gap_hbm, shift_hbm, cw_hbm, v_hbm, t_hbm, out_ref,
    order_ref, weight_ref, gap_ref, shift_ref, cw_ref, a_buf, v_buf, t_buf, vt,
    pole_b, weight_b, cau, part, precv, s1, r1, s2, r2, mz, cbuf,
    gf, gsum, gout, gin, gall, w1, w2, own_t, pf, ps, pr, pall,
    load_sem, pair_s, pair_r, s1_s, s1_r, s2_s, s2_r, z_sem, g_sem, gx_sem, p_sem, tok,
):
    z = lax.axis_index("row")
    c = lax.axis_index("col")
    core = c & 1
    q = c >> 1
    x, y = q & (NX - 1), q >> 2
    mate = (z, c + 1 - 2 * core)

    def zpeer(d):
        return (z + d + NZ) & (NZ - 1)

    def xchip(d):
        return (y * NX + ((x + d) & (NX - 1))) * 2 + core

    def ychip(d):
        return (((y + d) & (NY - 1)) * NX + x) * 2 + core

    def send(src, dst, ssem, rsem, dev):
        pltpu.make_async_remote_copy(
            src_ref=src, dst_ref=dst, send_sem=ssem, recv_sem=rsem, device_id=dev, device_id_type=MESH
        ).start()

    def wait(ref, sem):
        pltpu.make_async_copy(ref, ref, sem).wait()

    small = [
        (order_hbm, order_ref), (weight_hbm, weight_ref), (gap_hbm, gap_ref),
        (shift_hbm, shift_ref), (cw_hbm, cw_ref),
    ]
    for i, (src, dst) in enumerate(small):
        pltpu.make_async_copy(src, dst, load_sem.at[3 + i]).start()
    barrier = pltpu.get_barrier_semaphore()
    peers = [mate]
    for d in (1, 2, 3):
        peers += [(z, xchip(d)), (z, ychip(d))]
    peers += [(zpeer(d), c) for d in (1, -1)]
    for dev in peers:
        pl.semaphore_signal(barrier, inc=1, device_id=dev, device_id_type=MESH)

    for j, d in enumerate(DIST):
        pltpu.make_async_copy(a_hbm.at[zpeer(d)], a_buf.at[j // 4, :, j % 4], load_sem.at[0]).start()

    for i in range(4):
        wait(small[i][1], load_sem.at[3 + i])
    pltpu.make_async_copy(v_hbm, v_buf, load_sem.at[1]).start()
    pltpu.make_async_copy(t_hbm, t_buf, load_sem.at[2]).start()
    for b in range(4):
        lanes = pl.ds(b * 128, 128)
        pole = 2.0 * order_ref[:, lanes].astype(F32)
        pole_b[b] = jnp.broadcast_to(pole, (128, 128)).T
        weight_b[b] = jnp.broadcast_to(weight_ref[:, lanes], (128, 128)).T

    root = 2.0 * gap_ref[...].astype(F32) + 1.0 + shift_ref[...]
    turned_root = pltpu.roll(root, 64, 1)
    left1 = lax.broadcasted_iota(jnp.int32, (1, 128), 1) < 64

    def cauchy(n):
        for e in range(4):
            b0 = 2 * (4 * (n % 2) + e)
            if n < 2:
                lanes = jnp.where(left1, root[b0 : b0 + 1], turned_root[b0 + 1 : b0 + 2])
            else:
                lanes = jnp.where(left1, turned_root[b0 : b0 + 1], root[b0 + 1 : b0 + 2])
            for b in range(4):
                cau[n, b * 128 : b * 128 + 128, e * 128 : e * 128 + 128] = (
                    weight_b[b] / (pole_b[b] - lanes)
                ).astype(BF16)

    for n in range(4):
        cauchy(n)
    wait(a_buf, load_sem.at[0])
    for t in range(NT):
        for n in range(4):
            prod = dot(a_buf[t].reshape(128, 512), cau[n]).astype(BF16)
            for e in range(4):
                part[n // 2, t, 4 * (n % 2) + e] = prod[:, e * 128 : e * 128 + 128]
        if t == 0:
            pl.semaphore_wait(barrier, len(peers))
        send(part.at[1 - core, t], precv.at[t], pair_s, pair_r.at[t], mate)
    token(tok, 0, (1, -1), zpeer, c)

    wait(v_buf, load_sem.at[1])
    mine = pl.ds(pl.multiple_of(core * 128, 128), 128)
    gram = lax.dot_general(v_buf[1], v_buf[0, :, mine], TA, preferred_element_type=F32)
    gf[...] = gram.reshape(NQ, 16, 128)
    gsum[0] = gf[q]

    def gram_send(i):
        gout[i] = gsum[i].astype(BF16)
        for j in range(3):
            to = zpeer((1 - 2 * core) * (j + 1) * 4**i)
            send(gout.at[i], gin.at[i, j], g_sem.at[i], g_sem.at[2 + i], (to, c))

    def gram_add(i):
        wait(gin.at[i], g_sem.at[2 + i])
        gsum[i + 1] = gsum[i] + gin[i, 0].astype(F32) + gin[i, 1].astype(F32) + gin[i, 2].astype(F32)

    left64 = lax.broadcasted_iota(jnp.int32, (64, 128), 1) < 64

    def first_phase(t):
        wait(precv.at[t], pair_r.at[t])

        for yy in range(NY):
            for e in range(2):
                total = part[core, t, 2 * yy + e].astype(F32) + precv[t, 2 * yy + e].astype(F32)
                turned = pltpu.roll(total, 64, 1)
                even = jnp.where(left64, total[:64], turned[64:]).astype(BF16)
                odd = jnp.where(left64, turned[:64], total[64:]).astype(BF16)
                for xx, packed in ((2 * e, even), (2 * e + 1, odd)):
                    s1[t, 0, xx, yy] = packed[:32]
                    s1[t, 1, yy, xx] = packed[32:]

    def first_sends(t, ds):
        for d in ds:
            send(s1.at[t, 0, (x + d) & (NX - 1)], r1.at[t, 0, d - 1], s1_s, s1_r.at[t], (z, xchip(d)))
            send(s1.at[t, 1, (y + d) & (NY - 1)], r1.at[t, 1, d - 1], s1_s, s1_r.at[t], (z, ychip(d)))

    def second_phase(t):
        wait(r1.at[t], s1_r.at[t])
        for h, me in ((0, x), (1, y)):
            total = s1[t, h, me].astype(F32)
            for j in range(3):
                total += r1[t, h, j].astype(F32)
            s2[t, h] = total.astype(BF16)
        for d in (2, 1, 3):
            send(s2.at[t, 0, ((y + d) & (NY - 1))], r2.at[t, 0, d - 1], s2_s, s2_r.at[t], (z, ychip(d)))
            send(s2.at[t, 1, ((x + d) & (NX - 1))], r2.at[t, 1, d - 1], s2_s, s2_r.at[t], (z, xchip(d)))

    def exchange(t):
        wait(r2.at[t], s2_r.at[t])
        for h, me in ((0, y), (1, x)):
            total = s2[t, h, me].astype(F32)
            for j in range(3):
                total += r2[t, h, j].astype(F32)
            mz[t, 2 * h : 2 * h + 2] = (total * scale).astype(BF16).reshape(2, 16, 128)
        for i in range(4):
            d = DIST[4 * t + i]
            if d:
                send(mz.at[t, i], cbuf.at[z], z_sem.at[0], z_sem.at[1], (zpeer(d), c))
            else:
                cbuf[z] = mz[t, i]

    for t in range(3):
        first_phase(t)
        first_sends(t, (2, 1, 3))
    pl.semaphore_wait(tok.at[0], 2)
    token(tok, 1, (2, -2), zpeer, c)
    wait(cw_ref, load_sem.at[7])
    cw = cw_ref[pl.ds(q, 1), :]
    scale = jnp.where(lax.broadcasted_iota(jnp.int32, (1, 128), 1) // 64 == core, cw, pltpu.roll(cw, 64, 1))
    second_phase(0)
    first_phase(3)
    first_sends(3, (2, 1, 3))
    pl.semaphore_wait(tok.at[1], 2)
    token(tok, 2, (4, -4), zpeer, c)
    gram_send(0)
    second_phase(1)
    pl.semaphore_wait(tok.at[2], 2)
    exchange(0)
    second_phase(2)
    exchange(1)
    gram_add(0)
    gram_send(1)
    second_phase(3)
    exchange(2)
    exchange(3)
    for p in range(2):
        vt[p] = v_buf[p].T
    wait(t_buf, load_sem.at[2])
    w2[...] = lax.dot_general(t_buf[1].astype(BF16), vt[1], TA, preferred_element_type=F32).astype(BF16)

    wait(cbuf.at[pl.ds(0, NZ - 1)], z_sem.at[1])
    cur = cbuf[...].astype(F32)
    turned = pltpu.roll(cur.reshape(256, 128), 64, 1).reshape(NZ, 16, 128)
    left = lax.broadcasted_iota(jnp.int32, (NZ, 16, 128), 2) < 64
    own = jnp.stack([jnp.where(left, cur, turned), jnp.where(left, turned, cur)], axis=1).reshape(512, 128)
    own16 = own.astype(BF16)
    low = lax.broadcasted_iota(jnp.int32, (256, 128), 1) < 64
    proj = jnp.where(low, dot(vt[0], own16), dot(vt[1], own16)).reshape(8, 32, 128)
    pf[...] = proj
    ps[...] = proj.astype(BF16)
    slot = (z + 3) & (NZ - 1)
    for owner in OWNERS:

        @pl.when(z != owner)
        def _(owner=owner):
            send(
                ps.at[(owner + 3) % NZ], pr.at[(z - owner - 1 + NZ) & (NZ - 1)],
                p_sem.at[0], p_sem.at[1], (owner, c),
            )


    for b in range(4):
        own_t[:, b * 128 : b * 128 + 128] = own[b * 128 : b * 128 + 128].T[:64]
    gram_add(1)
    gall[core, q] = gsum[2].astype(BF16)
    for dy in range(NY):
        for dx in range(NX):
            if dx or dy:
                dest = (((y + dy) & (NY - 1)) * NX + ((x + dx) & (NX - 1))) * 2 + core
                send(gall.at[core, q], gall.at[core, q], g_sem.at[4], g_sem.at[5], (z, dest))

    @pl.when(slot < 8)
    def _():
        wait(pr, p_sem.at[1])
        total = pf[slot]
        for j in range(NZ - 1):
            total += pr[j].astype(F32)
        pall[slot] = total.astype(BF16)
        for dest in GATHER:

            @pl.when(z != dest)
            def _(dest=dest):
                send(pall.at[slot], pall.at[slot], p_sem.at[2], p_sem.at[3], (dest, c))

    wait(gall.at[0, pl.ds(0, NQ - 1)], g_sem.at[5])
    send(gall.at[core], gall.at[core], gx_sem.at[0], gx_sem.at[1], mate)
    wait(gall.at[0], gx_sem.at[1])
    rest = jnp.concatenate(
        [
            lax.dot_general(gall[k].reshape(256, 128), w2[...], TA, preferred_element_type=F32)
            for k in range(2)
        ],
        axis=0,
    )
    rest = (vt[0].astype(F32) - rest).astype(BF16)
    w1[...] = lax.dot_general(t_buf[0].astype(BF16), rest, TA, preferred_element_type=F32).astype(BF16)

    wait(precv, pair_s)
    wait(r1, s1_s)
    wait(r2, s2_s)
    for i in range(2):
        wait(gin.at[i], g_sem.at[i])
    wait(gall.at[0, pl.ds(0, NQ - 1)], g_sem.at[4])
    wait(gall.at[0], gx_sem.at[0])
    wait(cbuf.at[pl.ds(0, NZ - 1)], z_sem.at[0])

    @pl.when(slot < 8)
    def _():
        wait(pr.at[pl.ds(0, 7)], p_sem.at[0])
        wait(pall.at[pl.ds(0, 7)], p_sem.at[3])

    @pl.when(slot >= 8)
    def _():
        wait(pr.at[pl.ds(0, 8)], p_sem.at[0])
        wait(pall, p_sem.at[3])

    proj = pall[...].reshape(256, 128).T
    out_ref[...] = (own_t[...] - (dot(proj[:64], w1[...]) + dot(proj[64:], w2[...]))).astype(BF16)

    @pl.when(slot < 8)
    def _():
        wait(pr, p_sem.at[2])


def token(tok, at, steps, zpeer, c):
    for d in steps:
        pl.semaphore_signal(tok.at[at], inc=1, device_id=(zpeer(d), c), device_id_type=MESH)


def shards(a, order, weight, gap, shift, cw, v, t):
    hbm = pl.BlockSpec(memory_space=pl.ANY)
    dma = pltpu.SemaphoreType.DMA
    vmem = pltpu.VMEM
    out = pl.pallas_call(
        kernel,
        out_shape=vmem((64, 512), BF16),
        in_specs=[hbm] * 8,
        out_specs=pl.BlockSpec(memory_space=pltpu.VMEM),
        scratch_shapes=[
            vmem((1, 512), jnp.int32), vmem((1, 512), F32), vmem((NQ, 128), jnp.int32),
            vmem((NQ, 128), F32), vmem((NQ, 128), F32),
            vmem((NT, 2, 4, 16, 512), BF16),
            vmem((2, 512, 256), BF16),
            vmem((2, 256, 256), F32),
            vmem((2, 256, 512), BF16),
            vmem((4, 128, 128), F32),
            vmem((4, 128, 128), F32),
            vmem((4, 512, 512), BF16),
            vmem((2, NT, 8, 128, 128), BF16),
            vmem((NT, 8, 128, 128), BF16),
            vmem((NT, 2, 4, 4, 32, 128), BF16),
            vmem((NT, 2, 3, 4, 32, 128), BF16),
            vmem((NT, 2, 4, 32, 128), BF16),
            vmem((NT, 2, 3, 32, 128), BF16),
            vmem((NT, 4, 16, 128), BF16),
            vmem((NZ, 16, 128), BF16),
            vmem((NQ, 16, 128), F32),
            vmem((3, 16, 128), F32),
            vmem((2, 16, 128), BF16),
            vmem((2, 3, 16, 128), BF16),
            vmem((2, NQ, 16, 128), BF16),
            vmem((256, 512), BF16),
            vmem((256, 512), BF16),
            vmem((64, 512), F32),
            vmem((8, 32, 128), F32),
            vmem((8, 32, 128), BF16),
            vmem((NZ - 1, 32, 128), BF16),
            vmem((8, 32, 128), BF16),
            dma((8,)), dma, dma((NT,)), dma, dma((NT,)), dma, dma((NT,)),
            dma((2,)), dma((10,)), dma((2,)), dma((4,)), pltpu.SemaphoreType.REGULAR((3,)),
        ],
        compiler_params=pltpu.CompilerParams(collective_id=0, has_side_effects=True),
    )(
        a.reshape(NZ, 2, 16, 512), order.reshape(1, -1), weight.reshape(1, -1), gap.reshape(NQ, 128),
        shift.reshape(NQ, 128), cw.reshape(NQ, 128), v, t,
    )
    return out.T


def solution(mesh):
    return jax.shard_map(
        shards,
        mesh=mesh,
        in_specs=(P("row", "col"), P("col"), P("col"), P(), P(), P(), P(None, "row", None), P()),
        out_specs=P("row", "col"),
        check_vma=False,
    )
```
